512 devices in a mesh: chan: 32 (over y, z_lo, core), freq: 16 (over z_hi, x).
Axes of the slice: x: 4, y: 4, z: 16 (z_hi: 4, z_lo: 4; z = z_hi * 4 + z_lo), core: 2. Of those that a mesh axis runs over, the one named last changes fastest.
Arguments:
- spectra: bfloat16 [2, 30, 1024, 4096], P(None, None, 'freq', 'chan'), may hold values from -6 to 6
- src_ids: int32 [2, 32], replicated, may hold values from 0 to 4095
- pair_bin: int32 [2, 32, 4096], P(None, None, 'chan'), may hold values from 0 to 1023, as said below
- slot_of_bin: int32 [1024], replicated, may hold values from 0 to 1023, each once
Outputs:
- offset_gather: float32 [1024, 256], P('chan')
The draws below stay inside these ranges and needn't reach their ends.
Inputs may be any that keep to these rules, and one draw needn't show every extreme that they name: slot_of_bin names every row of offset_gather once. `pair_bin`: some offset bins are named by no pair.
All inputs are finite; a program needn't handle non-finite values.
Results may differ from the reference program's by a relative error of at most 0.0003.
Values may be sent and summed in bfloat16 or wider, within the bound.
A program may use at most 64 MiB of HBM per device.

```python
import math
import jax
import jax.numpy as jnp
from jax import lax

F = 1024
NLAG = 256
W = 30
NSRC = 32
STEPS = 2
CH = 4096
NBIN = 1024


def draw_pair_bin(key, part):
    empty_count = NBIN // 8
    used_count = NBIN - empty_count
    key_perm = jax.random.fold_in(key, 11)
    key_order = jax.random.fold_in(key, 12)
    key_coin = jax.random.fold_in(key, 13)
    key_outer = jax.random.fold_in(key, 14)
    key_inner = jax.random.fold_in(key, 15)
    key_flat = jax.random.fold_in(key, 16)
    inner_ids = (jax.random.permutation(key_perm, NBIN - 2) + 1).astype(jnp.int32)
    ends = jnp.array([0, NBIN - 1], jnp.int32)
    used_set = jnp.concatenate([ends, inner_ids[empty_count:]])
    used_ids = jax.random.permutation(key_order, used_set).astype(jnp.int32)
    shape = (STEPS, NSRC, CH)
    coin = jax.random.randint(key_coin, shape, 0, 2).astype(jnp.int32)
    outer = jax.random.randint(key_outer, shape, 1, used_count + 1).astype(jnp.int32)
    nested = jax.random.randint(key_inner, shape, 0, outer).astype(jnp.int32)
    flat_rank = jax.random.randint(key_flat, shape, 0, used_count).astype(jnp.int32)
    rank = jnp.where(coin == 0, nested, flat_rank)
    chosen = used_ids[rank].reshape(-1)
    chosen = chosen.at[0].set(NBIN - 1).at[1].set(0)
    return chosen.reshape(shape).astype(jnp.int32)


def set_ends(values, own_key, low, largest):
    shape = values.shape
    index_at = [jax.random.randint(jax.random.fold_in(own_key, axis), (), 0, shape[axis]) for axis in range(len(shape))]
    values = values.at[tuple(index_at)].set(low)
    longest = shape.index(max(shape))
    index_at[longest] = (index_at[longest] + 1) % shape[longest]
    return values.at[tuple(index_at)].set(largest)


def steps_of(stream_key, extent, cuts, low, top_value):
    factor_of, own = 1.0, jax.random.fold_in(stream_key, 6)
    for axis_at, parts in cuts:
        heights = jnp.exp(jax.random.uniform(jax.random.fold_in(own, axis_at), (parts,), jnp.float32, low / len(cuts), top_value / len(cuts)))
        factor_of = factor_of * jnp.repeat(heights, extent[axis_at] // parts).reshape([-1 if axis == axis_at else 1 for axis in range(len(extent))])
    return factor_of


def bell_draw(stream_key, extent, scale, limit, shards=(), kind=jnp.bfloat16):
    drawn = scale * jax.random.normal(stream_key, extent, jnp.float32)
    if shards:
        drawn = drawn * steps_of(stream_key, extent, shards, -0.22, 0.18)
    return jnp.clip(drawn, -limit, limit).astype(kind)


def setup_inputs(seed: int = 0) -> dict:
    arg_keys = jax.random.split(jax.random.key(seed), 5)
    spectra = bell_draw(arg_keys[0], (2, W, F, CH), 1.0, 6.0, ((2, 16), (3, 32)))
    src_ids = set_ends(jax.random.randint(arg_keys[1], (STEPS, NSRC), 0, CH), jax.random.fold_in(arg_keys[1], 1), 0, CH - 1).astype(jnp.int32)
    pair_bin = draw_pair_bin(jax.random.fold_in(arg_keys[4], 71), 0)
    slot_of_bin = jax.random.permutation(arg_keys[3], NBIN).astype(jnp.int32)
    return {"spectra": spectra, "src_ids": src_ids, "pair_bin": pair_bin, "slot_of_bin": slot_of_bin}


def lag_basis(anchor, amount, totals, lag_count, windows):
    frequency = anchor + lax.iota(jnp.int32, amount)
    shifts = lax.iota(jnp.int32, lag_count) - lag_count // 2
    phases = frequency[:, None] * shifts[None, :] % (2 * totals)
    angles = phases.astype(jnp.float32) * (math.pi / totals)
    factor = 1.0 / math.sqrt(windows * totals)
    return jnp.concatenate([jnp.cos(angles), -jnp.sin(angles)], axis=0) * factor

def reference(spectra, src_ids, pair_bin, slot_of_bin):
    span_f = min(F, 64)
    blocks = F // span_f
    lag_table = lag_basis(0, F, F, NLAG, W)
    binned = jnp.zeros((NBIN, 2 * F), jnp.float32)
    counts = jnp.zeros((NBIN,), jnp.float32)
    for step_no in range(STEPS):
        bin_ids = pair_bin[step_no].reshape(-1).astype(jnp.int32)
        source = spectra[:, :, :, src_ids[step_no]]

        def one_block(block_no):
            anchor = (block_no * span_f).astype(jnp.int32)
            receiver = lax.dynamic_slice_in_dim(spectra, anchor, span_f, 2).astype(jnp.float32)
            source_blk = lax.dynamic_slice_in_dim(source, anchor, span_f, 2).astype(jnp.float32)
            flipped = jnp.stack([-source_blk[1], source_blk[0]])
            stacked = jnp.stack([source_blk, flipped])
            crossed = jnp.einsum('jkwfs,kwfc->scjf', stacked, receiver)
            return jax.ops.segment_sum(crossed.reshape(NSRC * CH, 2 * span_f), bin_ids, num_segments=NBIN)
        pieces = lax.map(one_block, jnp.arange(blocks, dtype=jnp.int32))
        pieces = pieces.reshape(blocks, NBIN, 2, span_f).transpose(1, 2, 0, 3).reshape(NBIN, 2 * F)
        binned = binned + pieces
        counts = counts + jax.ops.segment_sum(jnp.ones((NSRC * CH,), jnp.float32), bin_ids, num_segments=NBIN)
    stacks = jnp.dot(binned, lag_table, precision=lax.Precision.HIGHEST)
    scaled = stacks / jnp.sqrt(jnp.maximum(counts, 1.0))[:, None]
    return jnp.zeros((NBIN, NLAG), jnp.float32).at[slot_of_bin].set(scaled)
```

```python
import math

import jax
import jax.numpy as jnp
from jax import lax
from jax.experimental import pallas as pl
from jax.experimental.pallas import tpu as pltpu
from jax.sharding import PartitionSpec as P

F = 1024
NLAG = 256
NBIN = 1024
W = 30
T = 2
NS = 32
FD = 64
C = 128
MESH = pl.DeviceIdType.MESH
BF = jnp.bfloat16
F32 = jnp.float32
NT = (((1,), (1,)), ((), ()))


def lag_basis(anchor, amount, totals, lag_count, windows):
    frequency = anchor + lax.iota(jnp.int32, amount)
    shifts = lax.iota(jnp.int32, lag_count) - lag_count // 2
    phases = frequency[:, None] * shifts[None, :] % (2 * totals)
    angles = phases.astype(jnp.float32) * (math.pi / totals)
    factor = 1.0 / math.sqrt(windows * totals)
    return jnp.concatenate([jnp.cos(angles), -jnp.sin(angles)], axis=0) * factor


def kernel(
    src_ref, spec_hbm, pair_ref, slot_ref, basis_ref, out_ref,
    spec, xf, bw, picker, pk, ck, rk, sk, slots, onehot, cnt, xs, xt, acc,
    bs, bc, br, lag, xr, zsum, zr, fin,
    in_sem, ck_s, ck_r, rk_s, rk_r, ag_s, ag_r, sc_s, sc_r,
    bc_s, bc_r, br_s, br_r, xr_s, xr_r, zr_s, zr_r, fx_s, fx_r,
):
    chan = lax.axis_index("chan")
    freq = lax.axis_index("freq")
    q = lax.div(chan, 2)
    k = lax.rem(chan, 2)
    y, z = lax.div(q, 4), lax.rem(q, 4)
    h, x = lax.div(freq, 4), lax.rem(freq, 4)
    core = {"chan": q * 2 + 1 - k, "freq": freq}

    def chip_at(o):
        return lax.rem(y + lax.div(o, 4), 4) * 4 + lax.rem(z + lax.rem(o, 4), 4)

    def chip_dev(o):
        return {"chan": chip_at(o) * 2 + k, "freq": freq}

    def x_dev(o):
        return {"chan": chan, "freq": h * 4 + lax.rem(x + o, 4)}

    def z_dev(o):
        return {"chan": chan, "freq": lax.rem(h + o, 4) * 4 + x}

    barrier = pltpu.get_barrier_semaphore()

    def greet(dev):
        pl.semaphore_signal(barrier, inc=1, device_id=dev, device_id_type=MESH)

    @pl.loop(1, 4)
    def _(o):
        greet(z_dev(o))
        greet(x_dev(o))

    @pl.loop(1, 16)
    def _(o):
        greet(chip_dev(o))

    greet(core)

    fetch = pltpu.make_async_copy(spec_hbm, spec, in_sem)
    fetch.start()

    lane = lax.broadcasted_iota(jnp.int32, (1, C), 1) + chan * C
    for t in range(T):
        for s in range(NS):
            row = t * NS + s
            picker[row : row + 1, :] = jnp.where(lane == src_ref[t, s], 1.0, 0.0)
    for part in range(2):
        xf[(part * 32 + W) * FD : (part + 1) * 32 * FD, :] = jnp.zeros((2 * FD, C), F32)
    fetch.wait()

    @pl.loop(0, W)
    def _(w):
        for part in range(2):
            at = pl.multiple_of((part * 32 + w) * FD, FD)
            xf[pl.ds(at, FD), :] = spec[part, w].astype(F32)

    pick = picker[...].astype(BF)

    @pl.loop(0, 32)
    def _(fp):
        for par in range(2):
            b = xf[pl.ds(par * 32 + fp, 64, stride=FD), :]
            bw[fp, par * 64 : par * 64 + 64, :C] = b.astype(BF)
            turned = jnp.concatenate([b[32:], -b[:32]], axis=0)
            bw[fp, par * 64 : par * 64 + 64, C:] = turned.astype(BF)
        got = lax.dot_general(pick, bw[fp, :, :C], NT, preferred_element_type=F32).astype(BF)
        for t in range(T):
            pk[t, fp] = got[t * NS : (t + 1) * NS]

    pl.semaphore_wait(barrier, 22)

    def core_src(t):
        return pltpu.make_async_remote_copy(
            src_ref=pk.at[t, pl.ds((1 - k) * 16, 16)], dst_ref=ck.at[t],
            send_sem=ck_s.at[t], recv_sem=ck_r.at[t], device_id=core, device_id_type=MESH)

    def scatter_src(t, o):
        return pltpu.make_async_remote_copy(
            src_ref=pk.at[t, k * 16 + chip_at(o)], dst_ref=rk.at[t, o],
            send_sem=rk_s.at[t, o], recv_sem=rk_r.at[t, o], device_id=chip_dev(o), device_id_type=MESH)

    def gather_src(t, o):
        return pltpu.make_async_remote_copy(
            src_ref=sk.at[t, k * 16 + q], dst_ref=sk.at[t, k * 16 + q],
            send_sem=ag_s.at[t, o], recv_sem=ag_r.at[t, o], device_id=chip_dev(o), device_id_type=MESH)

    def share_src(t):
        half = sk.at[t, pl.ds(k * 16, 16)]
        return pltpu.make_async_remote_copy(
            src_ref=half, dst_ref=half,
            send_sem=sc_s.at[t], recv_sem=sc_r.at[t], device_id=core, device_id_type=MESH)

    for t in range(T):
        core_src(t).start()
    for t in range(T):
        core_src(t).wait_recv()
        mine = pl.ds(k * 16, 16)
        pk[t, mine] = pk[t, mine] + ck[t]

        @pl.loop(1, 16)
        def _(o):
            scatter_src(t, o).start()

    bin_at = lax.broadcasted_iota(jnp.int32, (NBIN, 2 * C), 0)
    high = lax.broadcasted_iota(jnp.int32, (NBIN, 2 * C), 1) < C
    digits = jnp.where(high, lax.div(bin_at, 32), lax.rem(bin_at, 32)).astype(F32).astype(BF)

    @pl.loop(0, NBIN // C)
    def _(rb):
        rows = lax.broadcasted_iota(jnp.int32, (C, C), 0) + rb * C
        hit = jnp.concatenate(
            [jnp.where(slot_ref[i : i + 1, :] == rows, 1.0, 0.0).astype(BF) for i in range(NBIN // C)], axis=1)
        found = jnp.dot(hit, digits, preferred_element_type=F32)
        at = pl.ds(pl.multiple_of(rb * C, C), C)
        slots[at, :] = (found[:, :C] * 32.0 + found[:, C:]).astype(jnp.int32)
        cnt[at, :] = jnp.zeros((C, C), F32)

    def build_hits(t):
        @pl.loop(0, 4)
        def _(ch):
            @pl.loop(0, NBIN // C)
            def _(rb):
                at = pl.ds(pl.multiple_of(rb * C, C), C)
                held = slots[at, :]
                total = cnt[at, :]
                for i in range(8):
                    row = pair_ref[pl.ds(t * NS + ch * 8 + i, 1), :]
                    hit = jnp.where(held == row, 1.0, 0.0)
                    onehot[t * 4 + ch, at, i * C : (i + 1) * C] = hit.astype(BF)
                    total = total + hit
                cnt[at, :] = total

    def reduce_src(t):
        total = pk[t, k * 16 + q]
        for o in range(1, 16):
            scatter_src(t, o).wait_recv()
            total = total + rk[t, o]
        sk[t, k * 16 + q] = total

        @pl.loop(1, 16)
        def _(o):
            gather_src(t, o).start()

    build_hits(0)
    reduce_src(0)
    reduce_src(1)
    build_hits(1)

    sums = jnp.dot(cnt[...].astype(BF), jnp.ones((C, C), BF), preferred_element_type=F32)
    diagonal = lax.broadcasted_iota(jnp.int32, (32, C), 0) == lax.broadcasted_iota(jnp.int32, (32, C), 1)
    for owner in range(32):
        line = jnp.sum(jnp.where(diagonal, sums[owner * 32 : owner * 32 + 32], 0.0), axis=0, keepdims=True)
        bs[owner % 2, owner // 2, 32:40, :] = jnp.broadcast_to(line, (8, C))

    first = lax.broadcasted_iota(jnp.int32, (NS, C), 1) < 64

    def cross(t, fp):
        a = sk[t, fp]
        zero = jnp.zeros_like(a)
        lhs = jnp.concatenate([jnp.where(first, a, zero), jnp.where(first, zero, a)], axis=0)
        got = jnp.dot(lhs, bw[fp], preferred_element_type=F32)
        for par in range(2):
            for j in range(2):
                xs[pl.ds(j * FD + par * 32 + fp, NS, stride=2 * FD), :] = (
                    got[par * NS : (par + 1) * NS, j * C : (j + 1) * C])

    for t in range(T):
        @pl.loop(1, 16)
        def _(o):
            gather_src(t, o).wait_recv()

        share_src(t).start()

        @pl.loop(0, 16)
        def _(i):
            cross(t, k * 16 + i)

        share_src(t).wait_recv()

        @pl.loop(0, 16)
        def _(i):
            cross(t, (1 - k) * 16 + i)

        @pl.loop(0, 4)
        def _(ch):
            for i in range(8):
                at = pl.multiple_of((ch * 8 + i) * 2 * FD, 2 * FD)
                v = xs[pl.ds(at, 2 * FD), :]
                hi = v.astype(BF)
                xt[ch, :C, i * C : (i + 1) * C] = hi
                xt[ch, C:, i * C : (i + 1) * C] = (v - hi.astype(F32)).astype(BF)

        @pl.loop(0, 4)
        def _(ch):
            got = lax.dot_general(onehot[t * 4 + ch], xt[ch], NT, preferred_element_type=F32)
            if t == 0:
                @pl.when(ch == 0)
                def _():
                    acc[...] = got

                @pl.when(ch > 0)
                def _():
                    acc[...] += got
            else:
                acc[...] += got

    for owner in range(32):
        at = owner * 32
        bs[owner % 2, owner // 2, :32, :] = acc[at : at + 32, :C] + acc[at : at + 32, C:]

    core_bins = pltpu.make_async_remote_copy(
        src_ref=bs.at[1 - k], dst_ref=bc, send_sem=bc_s, recv_sem=bc_r, device_id=core, device_id_type=MESH)
    core_bins.start()
    core_bins.wait_recv()
    bs[k] = bs[k] + bc[...]

    def scatter_bins(o):
        return pltpu.make_async_remote_copy(
            src_ref=bs.at[k, chip_at(o)], dst_ref=br.at[o],
            send_sem=br_s.at[o], recv_sem=br_r.at[o], device_id=chip_dev(o), device_id_type=MESH)

    @pl.loop(1, 16)
    def _(o):
        scatter_bins(o).start()

    total = bs[k, q]
    for o in range(1, 16):
        scatter_bins(o).wait_recv()
        total = total + br[o]

    traces = jnp.dot(total[:32], basis_ref[...], precision=lax.Precision.HIGHEST, preferred_element_type=F32)
    for part in range(4):
        lag[part] = traces[part * 8 : part * 8 + 8]

    def scatter_x(o):
        return pltpu.make_async_remote_copy(
            src_ref=lag.at[lax.rem(x + o, 4)], dst_ref=xr.at[o],
            send_sem=xr_s.at[o], recv_sem=xr_r.at[o], device_id=x_dev(o), device_id_type=MESH)

    def swap_z(o):
        return pltpu.make_async_remote_copy(
            src_ref=zsum, dst_ref=zr.at[o],
            send_sem=zr_s.at[o], recv_sem=zr_r.at[o], device_id=z_dev(o), device_id_type=MESH)

    def gather_x(o):
        return pltpu.make_async_remote_copy(
            src_ref=fin.at[x], dst_ref=fin.at[x],
            send_sem=fx_s.at[o], recv_sem=fx_r.at[o], device_id=x_dev(o), device_id_type=MESH)

    for o in range(1, 4):
        scatter_x(o).start()
    rows = lag[x]
    for o in range(1, 4):
        scatter_x(o).wait_recv()
        rows = rows + xr[o]
    zsum[...] = rows
    for o in range(1, 4):
        swap_z(o).start()
    owned = (lax.broadcasted_iota(jnp.int32, (8, C), 1)
             == lax.broadcasted_iota(jnp.int32, (8, C), 0) + x * 8)
    counts = jnp.sum(jnp.where(owned, total[32:40], 0.0), axis=1, keepdims=True)
    norm = jnp.sqrt(jnp.maximum(counts, 1.0))
    for o in range(1, 4):
        swap_z(o).wait_recv()
        rows = rows + zr[o]
    fin[x] = rows / norm
    for o in range(1, 4):
        gather_x(o).start()

    for t in range(T):
        core_src(t).wait_send()
        share_src(t).wait_send()

        @pl.loop(1, 16)
        def _(o):
            scatter_src(t, o).wait_send()
            gather_src(t, o).wait_send()

    core_bins.wait_send()

    @pl.loop(1, 16)
    def _(o):
        scatter_bins(o).wait_send()

    for o in range(1, 4):
        scatter_x(o).wait_send()
        swap_z(o).wait_send()
    for o in range(1, 4):
        gather_x(o).wait()
    out_ref[...] = fin[...]


def body(spectra, src_ids, pair_bin, slot_of_bin):
    basis = lag_basis(lax.axis_index("freq") * FD, FD, F, NLAG, W)
    vmem = pl.BlockSpec(memory_space=pltpu.VMEM)
    dma = pltpu.SemaphoreType.DMA
    out = pl.pallas_call(
        kernel,
        out_shape=jax.ShapeDtypeStruct((4, 8, NLAG), F32),
        in_specs=[pl.BlockSpec(memory_space=pltpu.SMEM), pl.BlockSpec(memory_space=pl.ANY), vmem, vmem, vmem],
        out_specs=vmem,
        scratch_shapes=[
            pltpu.VMEM((2, W, FD, C), BF),
            pltpu.VMEM((64 * FD, C), F32),
            pltpu.VMEM((32, 2 * 64, 2 * C), BF),
            pltpu.VMEM((T * NS, C), F32),
            pltpu.VMEM((T, 32, NS, C), BF),
            pltpu.VMEM((T, 16, NS, C), BF),
            pltpu.VMEM((T, 16, NS, C), BF),
            pltpu.VMEM((T, 32, NS, C), BF),
            pltpu.VMEM((NBIN, C), jnp.int32),
            pltpu.VMEM((8, NBIN, 8 * C), BF),
            pltpu.VMEM((NBIN, C), F32),
            pltpu.VMEM((NS * 2 * FD, C), F32),
            pltpu.VMEM((4, 2 * C, 8 * C), BF),
            pltpu.VMEM((NBIN, 2 * C), F32),
            pltpu.VMEM((2, 16, 40, C), F32),
            pltpu.VMEM((16, 40, C), F32),
            pltpu.VMEM((16, 40, C), F32),
            pltpu.VMEM((4, 8, NLAG), F32),
            pltpu.VMEM((4, 8, NLAG), F32),
            pltpu.VMEM((8, NLAG), F32),
            pltpu.VMEM((4, 8, NLAG), F32),
            pltpu.VMEM((4, 8, NLAG), F32),
            dma, dma((T,)), dma((T,)), dma((T, 16)), dma((T, 16)), dma((T, 16)), dma((T, 16)), dma((T,)), dma((T,)),
            dma, dma, dma((16,)), dma((16,)), dma((4,)), dma((4,)), dma((4,)), dma((4,)), dma((4,)), dma((4,)),
        ],
        compiler_params=pltpu.CompilerParams(
            collective_id=0, has_side_effects=True, vmem_limit_bytes=56 * 1024 * 1024),
    )(src_ids, spectra, pair_bin.reshape(T * NS, C), slot_of_bin.reshape(NBIN // C, C), basis)
    return out.reshape(32, NLAG)


def solution(mesh):
    return jax.shard_map(
        body,
        mesh=mesh,
        in_specs=(P(None, None, "freq", "chan"), P(), P(None, None, "chan"), P()),
        out_specs=P("chan", None),
        check_vma=False,
    )
```

```python
import math

import jax
import jax.numpy as jnp
from jax import lax
from jax.experimental import pallas as pl
from jax.experimental.pallas import tpu as pltpu
from jax.sharding import PartitionSpec as P

F = 1024
NLAG = 256
NBIN = 1024
W = 30
T = 2
NS = 32
FD = 64
C = 128
MESH = pl.DeviceIdType.MESH
BF = jnp.bfloat16
F32 = jnp.float32
NT = (((1,), (1,)), ((), ()))


def kernel(
    src_ref, spec_hbm, pair_ref, slot_ref, out_ref, norm_ref,
    spec, xf, bw, bt, picker, pk, ck, rk, sk, slots, onehot, cnt, xs, xt, basis,
    bs, bc, br, lag, xr, zsum, zr, fin,
    in_sem, ck_s, ck_r, rk_s, rk_r, ag_s, ag_r, sc_s, sc_r,
    bc_s, bc_r, br_s, br_r, xr_s, xr_r, zr_s, zr_r, fx_s, fx_r,
):
    chan = lax.axis_index("chan")
    freq = lax.axis_index("freq")
    q = lax.div(chan, 2)
    k = lax.rem(chan, 2)
    y, z = lax.div(q, 4), lax.rem(q, 4)
    h, x = lax.div(freq, 4), lax.rem(freq, 4)
    core = {"chan": q * 2 + 1 - k, "freq": freq}

    def chip_at(o):
        return lax.rem(y + lax.div(o, 4), 4) * 4 + lax.rem(z + lax.rem(o, 4), 4)

    def chip_from(o):
        return lax.rem(y + 4 - lax.div(o, 4), 4) * 4 + lax.rem(z + 4 - lax.rem(o, 4), 4)

    def chip_dev(o):
        return {"chan": chip_at(o) * 2 + k, "freq": freq}

    def x_dev(o):
        return {"chan": chan, "freq": h * 4 + lax.rem(x + o, 4)}

    def z_dev(o):
        return {"chan": chan, "freq": lax.rem(h + o, 4) * 4 + x}

    barrier = pltpu.get_barrier_semaphore()

    def greet(dev):
        pl.semaphore_signal(barrier, inc=1, device_id=dev, device_id_type=MESH)

    @pl.loop(1, 4)
    def _(o):
        greet(z_dev(o))
        greet(x_dev(o))

    @pl.loop(1, 16)
    def _(o):
        greet(chip_dev(o))

    greet(core)

    fetch = pltpu.make_async_copy(spec_hbm, spec, in_sem)
    fetch.start()

    lane = lax.broadcasted_iota(jnp.int32, (1, C), 1) + chan * C
    for t in range(T):
        for s in range(NS):
            row = t * NS + s
            picker[row : row + 1, :] = jnp.where(lane == src_ref[t, s], 1.0, 0.0)
    for part in range(2):
        xf[(part * 32 + W) * FD : (part + 1) * 32 * FD, :] = jnp.zeros((2 * FD, C), F32)
    fetch.wait()

    @pl.loop(0, W, unroll=5)
    def _(w):
        for part in range(2):
            at = pl.multiple_of((part * 32 + w) * FD, FD)
            xf[pl.ds(at, FD), :] = spec[part, w].astype(F32)

    pick = picker[...].astype(BF)

    @pl.loop(0, 32, unroll=8)
    def _(fp):
        halves = [xf[pl.ds(par * 32 + fp, 64, stride=FD), :].astype(BF) for par in range(2)]
        b = jnp.concatenate(halves, axis=0)
        bw[fp] = b
        got = lax.dot_general(pick, b, NT, preferred_element_type=F32).astype(BF)
        for t in range(T):
            pk[t, fp] = got[t * NS : (t + 1) * NS]

    pl.semaphore_wait(barrier, 22)

    def core_src(t):
        return pltpu.make_async_remote_copy(
            src_ref=pk.at[t, pl.ds((1 - k) * 16, 16)], dst_ref=ck.at[t],
            send_sem=ck_s.at[t], recv_sem=ck_r.at[t], device_id=core, device_id_type=MESH)

    def scatter_src(t, o):
        return pltpu.make_async_remote_copy(
            src_ref=pk.at[t, k * 16 + chip_at(o)], dst_ref=rk.at[t, o],
            send_sem=rk_s.at[t, o], recv_sem=rk_r.at[t, o], device_id=chip_dev(o), device_id_type=MESH)

    def gather_src(t, o):
        return pltpu.make_async_remote_copy(
            src_ref=sk.at[t, k * 16 + q], dst_ref=sk.at[t, k * 16 + q],
            send_sem=ag_s.at[t, o], recv_sem=ag_r.at[t, o], device_id=chip_dev(o), device_id_type=MESH)

    def share_src(t, o, half):
        at = half * 16 + chip_from(o)
        return pltpu.make_async_remote_copy(
            src_ref=sk.at[t, at], dst_ref=sk.at[t, at],
            send_sem=sc_s.at[t, o], recv_sem=sc_r.at[t, o], device_id=core, device_id_type=MESH)

    for t in range(T):
        core_src(t).start()
    for t in range(T):
        core_src(t).wait_recv()
        mine = pl.ds(k * 16, 16)
        pk[t, mine] = pk[t, mine] + ck[t]

        @pl.loop(1, 16)
        def _(o):
            scatter_src(t, o).start()

    @pl.loop(0, 32, unroll=4)
    def _(fp):
        for par in range(2):
            at = par * 64
            bt[fp, at : at + 32] = bw[fp, at + 32 : at + 64]
            bt[fp, at + 32 : at + 64] = -bw[fp, at : at + 32]

    bin_at = lax.broadcasted_iota(jnp.int32, (NBIN, 2 * C), 0)
    high = lax.broadcasted_iota(jnp.int32, (NBIN, 2 * C), 1) < C
    digits = jnp.where(high, lax.div(bin_at, 32), lax.rem(bin_at, 32)).astype(F32).astype(BF)

    @pl.loop(0, NBIN // C)
    def _(rb):
        at = lax.broadcasted_iota(jnp.int32, (C, C), 0) + rb * C
        rows = lax.div(lax.rem(at, 512), 32) * 64 + lax.div(at, 512) * 32 + lax.rem(at, 32)
        hit = jnp.concatenate(
            [jnp.where(slot_ref[i : i + 1, :] == rows, 1.0, 0.0).astype(BF) for i in range(NBIN // C)], axis=1)
        found = jnp.dot(hit, digits, preferred_element_type=F32)
        at = pl.ds(pl.multiple_of(rb * C, C), C)
        slots[at, :] = (found[:, :C] * 32.0 + found[:, C:]).astype(jnp.int32)
        cnt[at, :] = jnp.zeros((C, C), F32)

    def build_hits(t):
        @pl.loop(0, 4)
        def _(ch):
            @pl.loop(0, NBIN // C)
            def _(rb):
                at = pl.ds(pl.multiple_of(rb * C, C), C)
                held = slots[at, :]
                total = cnt[at, :]
                for i in range(8):
                    row = pair_ref[pl.ds(t * NS + ch * 8 + i, 1), :]
                    hit = jnp.where(held == row, 1.0, 0.0)
                    onehot[t * 4 + ch, at, i * C : (i + 1) * C] = hit.astype(BF)
                    total = total + hit
                cnt[at, :] = total

    def reduce_src(t):
        total = pk[t, k * 16 + q]
        for o in range(1, 16):
            scatter_src(t, o).wait_recv()
            total = total + rk[t, o]
        sk[t, k * 16 + q] = total

        @pl.loop(1, 16)
        def _(o):
            gather_src(t, o).start()

    build_hits(0)
    reduce_src(0)
    reduce_src(1)
    build_hits(1)

    sums = jnp.dot(cnt[...].astype(BF), jnp.ones((C, C), BF), preferred_element_type=F32)
    diagonal = lax.broadcasted_iota(jnp.int32, (32, C), 0) == lax.broadcasted_iota(jnp.int32, (32, C), 1)
    for owner in range(32):
        line = jnp.sum(jnp.where(diagonal, sums[owner * 32 : owner * 32 + 32], 0.0), axis=0, keepdims=True)
        bs[owner // 16, owner % 16, 32:40, :] = jnp.broadcast_to(line, (8, C))

    tone = lax.broadcasted_iota(jnp.int32, (FD, NLAG), 0) + freq * FD
    shift = lax.broadcasted_iota(jnp.int32, (FD, NLAG), 1) - NLAG // 2
    angles = ((tone * shift) & (2 * F - 1)).astype(F32) * (math.pi / F)
    factor = 1.0 / math.sqrt(W * F)
    basis[:FD, :] = jnp.cos(angles) * factor
    basis[FD:, :] = -jnp.sin(angles) * factor

    first = lax.broadcasted_iota(jnp.int32, (NS, C), 1) < 64

    def cross(t, fp):
        a = sk[t, fp]
        zero = jnp.zeros_like(a)
        lhs = jnp.concatenate([jnp.where(first, a, zero), jnp.where(first, zero, a)], axis=0)
        got = jnp.dot(lhs, jnp.concatenate([bw[fp], bt[fp]], axis=1), preferred_element_type=F32)
        for par in range(2):
            for j in range(2):
                xs[pl.ds(j * FD + par * 32 + fp, NS, stride=2 * FD), :] = (
                    got[par * NS : (par + 1) * NS, j * C : (j + 1) * C])

    core_bins = pltpu.make_async_remote_copy(
        src_ref=bs.at[1 - k], dst_ref=bc, send_sem=bc_s, recv_sem=bc_r, device_id=core, device_id_type=MESH)

    for t in range(T):
        share_src(t, 0, k).start()
        for group in range(4):
            members = range(group * 4, group * 4 + 4)
            for o in members:
                if o > 0:
                    gather_src(t, o).wait_recv()
                    share_src(t, o, k).start()
            for o in members:
                cross(t, k * 16 + chip_from(o))
        for group in range(2):
            members = range(group * 8, group * 8 + 8)
            for o in members:
                share_src(t, o, 1 - k).wait_recv()
            for o in members:
                cross(t, (1 - k) * 16 + chip_from(o))

        for ch in range(4):
            for i in range(8):
                at = (ch * 8 + i) * 2 * FD
                v = xs[at : at + 2 * FD, :]
                hi = v.astype(BF)
                xt[ch, :C, i * C : (i + 1) * C] = hi
                xt[ch, C:, i * C : (i + 1) * C] = (v - hi.astype(F32)).astype(BF)

        for half in (1 - k, k):
            at = pl.ds(pl.multiple_of(half * 512, 512), 512)
            got = sum(
                lax.dot_general(onehot[t * 4 + ch, at, :], xt[ch], NT, preferred_element_type=F32) for ch in range(4))
            part = (got[:, :C] + got[:, C:]).reshape(16, 32, C)
            if t == 0:
                bs[half, :, :32, :] = part
            else:
                bs[half, :, :32, :] = bs[half, :, :32, :] + part
                if half is not k:
                    core_bins.start()

    core_bins.wait_recv()
    bs[k] = bs[k] + bc[...]

    def scatter_bins(o):
        return pltpu.make_async_remote_copy(
            src_ref=bs.at[k, chip_at(o)], dst_ref=br.at[o],
            send_sem=br_s.at[o], recv_sem=br_r.at[o], device_id=chip_dev(o), device_id_type=MESH)

    @pl.loop(1, 16)
    def _(o):
        scatter_bins(o).start()

    total = bs[k, q]
    for o in range(1, 16):
        scatter_bins(o).wait_recv()
        total = total + br[o]

    traces = jnp.dot(total[:32], basis[...], precision=lax.Precision.HIGHEST, preferred_element_type=F32)
    for part in range(4):
        lag[part] = traces[part * 8 : part * 8 + 8]

    def scatter_x(o):
        return pltpu.make_async_remote_copy(
            src_ref=lag.at[lax.rem(x + o, 4)], dst_ref=xr.at[o],
            send_sem=xr_s.at[o], recv_sem=xr_r.at[o], device_id=x_dev(o), device_id_type=MESH)

    def swap_z(o):
        return pltpu.make_async_remote_copy(
            src_ref=zsum, dst_ref=zr.at[o],
            send_sem=zr_s.at[o], recv_sem=zr_r.at[o], device_id=z_dev(o), device_id_type=MESH)

    def gather_x(o):
        return pltpu.make_async_remote_copy(
            src_ref=fin.at[x], dst_ref=fin.at[x],
            send_sem=fx_s.at[o], recv_sem=fx_r.at[o], device_id=x_dev(o), device_id_type=MESH)

    for o in range(1, 4):
        scatter_x(o).start()
    rows = lag[x]
    for o in range(1, 4):
        scatter_x(o).wait_recv()
        rows = rows + xr[o]
    zsum[...] = rows
    for o in range(1, 4):
        swap_z(o).start()
    counts = jnp.sum(jnp.where(diagonal, total[32:33], 0.0), axis=1, keepdims=True)
    norm_ref[...] = jnp.broadcast_to(jnp.sqrt(jnp.maximum(counts, 1.0)), (32, NLAG))
    for o in range(1, 4):
        swap_z(o).wait_recv()
        rows = rows + zr[o]
    fin[x] = rows
    for o in range(1, 4):
        gather_x(o).start()

    for t in range(T):
        core_src(t).wait_send()
        share_src(t, 0, k).wait_send()

        @pl.loop(1, 16)
        def _(o):
            share_src(t, o, k).wait_send()
            scatter_src(t, o).wait_send()
            gather_src(t, o).wait_send()

    core_bins.wait_send()

    @pl.loop(1, 16)
    def _(o):
        scatter_bins(o).wait_send()

    for o in range(1, 4):
        scatter_x(o).wait_send()
        swap_z(o).wait_send()
    for o in range(1, 4):
        gather_x(o).wait()
    out_ref[...] = fin[...]


def body(spectra, src_ids, pair_bin, slot_of_bin):
    vmem = pl.BlockSpec(memory_space=pltpu.VMEM)
    dma = pltpu.SemaphoreType.DMA
    sums, norm = pl.pallas_call(
        kernel,
        out_shape=[jax.ShapeDtypeStruct((4, 8, NLAG), F32), jax.ShapeDtypeStruct((32, NLAG), F32)],
        in_specs=[pl.BlockSpec(memory_space=pltpu.SMEM), pl.BlockSpec(memory_space=pl.ANY), vmem, vmem],
        out_specs=[vmem, vmem],
        scratch_shapes=[
            pltpu.VMEM((2, W, FD, C), BF),
            pltpu.VMEM((64 * FD, C), F32),
            pltpu.VMEM((32, 2 * 64, C), BF),
            pltpu.VMEM((32, 2 * 64, C), BF),
            pltpu.VMEM((T * NS, C), F32),
            pltpu.VMEM((T, 32, NS, C), BF),
            pltpu.VMEM((T, 16, NS, C), BF),
            pltpu.VMEM((T, 16, NS, C), BF),
            pltpu.VMEM((T, 32, NS, C), BF),
            pltpu.VMEM((NBIN, C), jnp.int32),
            pltpu.VMEM((8, NBIN, 8 * C), BF),
            pltpu.VMEM((NBIN, C), F32),
            pltpu.VMEM((NS * 2 * FD, C), F32),
            pltpu.VMEM((4, 2 * C, 8 * C), BF),
            pltpu.VMEM((2 * FD, NLAG), F32),
            pltpu.VMEM((2, 16, 40, C), F32),
            pltpu.VMEM((16, 40, C), F32),
            pltpu.VMEM((16, 40, C), F32),
            pltpu.VMEM((4, 8, NLAG), F32),
            pltpu.VMEM((4, 8, NLAG), F32),
            pltpu.VMEM((8, NLAG), F32),
            pltpu.VMEM((4, 8, NLAG), F32),
            pltpu.VMEM((4, 8, NLAG), F32),
            dma, dma((T,)), dma((T,)), dma((T, 16)), dma((T, 16)), dma((T, 16)), dma((T, 16)), dma((T, 16)), dma((T, 16)),
            dma, dma, dma((16,)), dma((16,)), dma((4,)), dma((4,)), dma((4,)), dma((4,)), dma((4,)), dma((4,)),
        ],
        compiler_params=pltpu.CompilerParams(
            collective_id=0, has_side_effects=True, vmem_limit_bytes=56 * 1024 * 1024),
    )(src_ids, spectra, pair_bin.reshape(T * NS, C), slot_of_bin.reshape(NBIN // C, C))
    return sums.reshape(32, NLAG) / norm


def solution(mesh):
    return jax.shard_map(
        body,
        mesh=mesh,
        in_specs=(P(None, None, "freq", "chan"), P(), P(None, None, "chan"), P()),
        out_specs=P("chan", None),
        check_vma=False,
    )
```

```python
import math

import jax
import jax.numpy as jnp
from jax import lax
from jax.experimental import pallas as pl
from jax.experimental.pallas import tpu as pltpu
from jax.sharding import PartitionSpec as P

F = 1024
NLAG = 256
NBIN = 1024
W = 30
T = 2
NS = 32
FD = 64
C = 128
MESH = pl.DeviceIdType.MESH
BF = jnp.bfloat16
F32 = jnp.float32
NT = (((1,), (1,)), ((), ()))


def kernel(
    src_ref, spec_hbm, pair_ref, slot_ref, out_ref, norm_ref,
    spec, xf, bw, bt, picker, pk, ck, rk, sk, slots, onehot, cnt, xs, xt, basis,
    bs, bc, br, lag, xr, zsum, zr, fin,
    in_sem, ck_s, ck_r, rk_s, rk_r, ag_s, ag_r, sc_s, sc_r,
    bc_s, bc_r, br_s, br_r, xr_s, xr_r, zr_s, zr_r, fx_s, fx_r,
):
    chan = lax.axis_index("chan")
    freq = lax.axis_index("freq")
    q = lax.div(chan, 2)
    k = lax.rem(chan, 2)
    y, z = lax.div(q, 4), lax.rem(q, 4)
    h, x = lax.div(freq, 4), lax.rem(freq, 4)
    core = {"chan": q * 2 + 1 - k, "freq": freq}

    def chip_at(o):
        return lax.rem(y + lax.div(o, 4), 4) * 4 + lax.rem(z + lax.rem(o, 4), 4)

    def chip_from(o):
        return lax.rem(y + 4 - lax.div(o, 4), 4) * 4 + lax.rem(z + 4 - lax.rem(o, 4), 4)

    def chip_dev(o):
        return {"chan": chip_at(o) * 2 + k, "freq": freq}

    def x_dev(o):
        return {"chan": chan, "freq": h * 4 + lax.rem(x + o, 4)}

    def z_dev(o):
        return {"chan": chan, "freq": lax.rem(h + o, 4) * 4 + x}

    barrier = pltpu.get_barrier_semaphore()

    def greet(dev):
        pl.semaphore_signal(barrier, inc=1, device_id=dev, device_id_type=MESH)

    @pl.loop(1, 4)
    def _(o):
        greet(z_dev(o))
        greet(x_dev(o))

    @pl.loop(1, 16)
    def _(o):
        greet(chip_dev(o))

    greet(core)

    fetch = pltpu.make_async_copy(spec_hbm, spec, in_sem)
    fetch.start()

    lane = lax.broadcasted_iota(jnp.int32, (1, C), 1) + chan * C
    for t in range(T):
        for s in range(NS):
            row = t * NS + s
            picker[row : row + 1, :] = jnp.where(lane == src_ref[t, s], 1.0, 0.0)
    for part in range(2):
        xf[(part * 32 + W) * FD : (part + 1) * 32 * FD, :] = jnp.zeros((2 * FD, C), F32)
    fetch.wait()

    @pl.loop(0, W, unroll=5)
    def _(w):
        for part in range(2):
            at = pl.multiple_of((part * 32 + w) * FD, FD)
            xf[pl.ds(at, FD), :] = spec[part, w].astype(F32)

    pick = picker[...].astype(BF)

    @pl.loop(0, 32, unroll=8)
    def _(fp):
        halves = [xf[pl.ds(par * 32 + fp, 64, stride=FD), :].astype(BF) for par in range(2)]
        b = jnp.concatenate(halves, axis=0)
        bw[fp] = b
        got = lax.dot_general(pick, b, NT, preferred_element_type=F32).astype(BF)
        for t in range(T):
            pk[t, fp] = got[t * NS : (t + 1) * NS]

    pl.semaphore_wait(barrier, 22)

    def core_src(t):
        return pltpu.make_async_remote_copy(
            src_ref=pk.at[t, pl.ds((1 - k) * 16, 16)], dst_ref=ck.at[t],
            send_sem=ck_s.at[t], recv_sem=ck_r.at[t], device_id=core, device_id_type=MESH)

    def scatter_src(t, o):
        return pltpu.make_async_remote_copy(
            src_ref=pk.at[t, k * 16 + chip_at(o)], dst_ref=rk.at[t, o],
            send_sem=rk_s.at[t, o], recv_sem=rk_r.at[t, o], device_id=chip_dev(o), device_id_type=MESH)

    def gather_src(t, o):
        return pltpu.make_async_remote_copy(
            src_ref=sk.at[t, k * 16 + q], dst_ref=sk.at[t, k * 16 + q],
            send_sem=ag_s.at[t, o], recv_sem=ag_r.at[t, o], device_id=chip_dev(o), device_id_type=MESH)

    def share_src(t, o, half):
        at = half * 16 + chip_from(o)
        return pltpu.make_async_remote_copy(
            src_ref=sk.at[t, at], dst_ref=sk.at[t, at],
            send_sem=sc_s.at[t, o], recv_sem=sc_r.at[t, o], device_id=core, device_id_type=MESH)

    for t in range(T):
        core_src(t).start()
    for t in range(T):
        core_src(t).wait_recv()
        mine = pl.ds(k * 16, 16)
        pk[t, mine] = pk[t, mine] + ck[t]

        @pl.loop(1, 16)
        def _(o):
            scatter_src(t, o).start()

    @pl.loop(0, 32, unroll=4)
    def _(fp):
        for par in range(2):
            at = par * 64
            bt[fp, at : at + 32] = bw[fp, at + 32 : at + 64]
            bt[fp, at + 32 : at + 64] = -bw[fp, at : at + 32]

    bin_at = lax.broadcasted_iota(jnp.int32, (NBIN, 2 * C), 0)
    high = lax.broadcasted_iota(jnp.int32, (NBIN, 2 * C), 1) < C
    digits = jnp.where(high, lax.div(bin_at, 32), lax.rem(bin_at, 32)).astype(F32).astype(BF)

    @pl.loop(0, NBIN // C)
    def _(rb):
        at = lax.broadcasted_iota(jnp.int32, (C, C), 0) + rb * C
        chip = lax.div(lax.rem(at, 256), 32) * 2 + lax.div(lax.rem(at, 512), 256)
        rows = chip * 64 + lax.div(at, 512) * 32 + lax.rem(at, 32)
        hit = jnp.concatenate(
            [jnp.where(slot_ref[i : i + 1, :] == rows, 1.0, 0.0).astype(BF) for i in range(NBIN // C)], axis=1)
        found = jnp.dot(hit, digits, preferred_element_type=F32)
        at = pl.ds(pl.multiple_of(rb * C, C), C)
        slots[at, :] = (found[:, :C] * 32.0 + found[:, C:]).astype(jnp.int32)
        cnt[at, :] = jnp.zeros((C, C), BF)

    def build_hits(t):
        @pl.loop(0, 4)
        def _(ch):
            @pl.loop(0, NBIN // C)
            def _(rb):
                at = pl.ds(pl.multiple_of(rb * C, C), C)
                held = slots[at, :]
                total = cnt[at, :]
                for i in range(8):
                    row = pair_ref[pl.ds(t * NS + ch * 8 + i, 1), :]
                    hit = jnp.where(held == row, 1.0, 0.0).astype(BF)
                    onehot[t * 4 + ch, at, i * C : (i + 1) * C] = hit
                    total = total + hit
                cnt[at, :] = total

    def reduce_src(t):
        total = pk[t, k * 16 + q]
        for o in range(1, 16):
            scatter_src(t, o).wait_recv()
            total = total + rk[t, o]
        sk[t, k * 16 + q] = total

        @pl.loop(1, 16)
        def _(o):
            gather_src(t, o).start()

    build_hits(0)
    reduce_src(0)
    reduce_src(1)
    build_hits(1)

    sums = jnp.dot(cnt[...], jnp.ones((C, C), BF), preferred_element_type=F32)
    diagonal = lax.broadcasted_iota(jnp.int32, (32, C), 0) == lax.broadcasted_iota(jnp.int32, (32, C), 1)
    for owner in range(32):
        line = jnp.sum(jnp.where(diagonal, sums[owner * 32 : owner * 32 + 32], 0.0), axis=0, keepdims=True)
        bs[owner // 16, owner // 8 % 2, owner % 8, 32:33, :] = line

    first = lax.broadcasted_iota(jnp.int32, (NS, C), 1) < 64

    def cross(t, fp):
        a = sk[t, fp]
        zero = jnp.zeros_like(a)
        lhs = jnp.concatenate([jnp.where(first, a, zero), jnp.where(first, zero, a)], axis=0)
        got = jnp.dot(lhs, jnp.concatenate([bw[fp], bt[fp]], axis=1), preferred_element_type=F32)
        for par in range(2):
            for j in range(2):
                xs[pl.ds(j * FD + par * 32 + fp, NS, stride=2 * FD), :] = (
                    got[par * NS : (par + 1) * NS, j * C : (j + 1) * C])

    def core_bins(g):
        return pltpu.make_async_remote_copy(
            src_ref=bs.at[1 - k, g], dst_ref=bc.at[g],
            send_sem=bc_s.at[g], recv_sem=bc_r.at[g], device_id=core, device_id_type=MESH)

    def scatter_bins(o):
        to = chip_at(o)
        return pltpu.make_async_remote_copy(
            src_ref=bs.at[k, lax.rem(to, 2), lax.div(to, 2)], dst_ref=br.at[o],
            send_sem=br_s.at[o], recv_sem=br_r.at[o], device_id=chip_dev(o), device_id_type=MESH)

    def split(t):
        for ch in range(4):
            for i in range(8):
                at = (ch * 8 + i) * 2 * FD
                v = xs[at : at + 2 * FD, :]
                hi = v.astype(BF)
                xt[ch, :C, i * C : (i + 1) * C] = hi
                xt[ch, C:, i * C : (i + 1) * C] = (v - hi.astype(F32)).astype(BF)

    def stack(t, start, rows):
        at = pl.ds(start, rows)
        got = sum(
            lax.dot_general(onehot[t * 4 + ch, at, :], xt[ch], NT, preferred_element_type=F32) for ch in range(4))
        return (got[:, :C] + got[:, C:]).reshape(rows // 32, 32, C)

    share_src(0, 0, k).start()
    for group in range(4):
        members = range(group * 4, group * 4 + 4)
        for o in members:
            if o > 0:
                gather_src(0, o).wait_recv()
                share_src(0, o, k).start()
        for o in members:
            cross(0, k * 16 + chip_from(o))
    for group in range(2):
        members = range(group * 8, group * 8 + 8)
        for o in members:
            share_src(0, o, 1 - k).wait_recv()
        for o in members:
            cross(0, (1 - k) * 16 + chip_from(o))

    share_src(1, 0, k).start()

    @pl.loop(1, 16)
    def _(o):
        gather_src(1, o).wait_recv()
        share_src(1, o, k).start()

    split(0)
    part = stack(0, 0, NBIN)
    for n in range(4):
        bs[n // 2, n % 2, :, :32, :] = part[n * 8 : n * 8 + 8]

    for o in range(16):
        cross(1, k * 16 + chip_from(o))

    @pl.loop(0, 16)
    def _(o):
        share_src(1, o, 1 - k).wait_recv()

    for o in range(16):
        cross(1, (1 - k) * 16 + chip_from(o))
    split(1)

    def stack_on(half, g):
        part = stack(1, pl.multiple_of(half * 512 + g * 256, 256), 256)
        bs[half, g, :, :32, :] = bs[half, g, :, :32, :] + part

    for g in range(2):
        stack_on(1 - k, g)
        core_bins(g).start()
        stack_on(k, g)
        core_bins(g).wait_recv()
        bs[k, g] = bs[k, g] + bc[g]

        @pl.loop(0, 8)
        def _(n):
            o = lax.div(n, 2) * 4 + lax.rem(n, 2) * 2 + lax.rem(z + g, 2)

            @pl.when(o > 0)
            def _():
                scatter_bins(o).start()

    tone = lax.broadcasted_iota(jnp.int32, (FD, NLAG), 0) + freq * FD
    shift = lax.broadcasted_iota(jnp.int32, (FD, NLAG), 1) - NLAG // 2
    angles = ((tone * shift) & (2 * F - 1)).astype(F32) * (math.pi / F)
    factor = 1.0 / math.sqrt(W * F)
    basis[:FD, :] = jnp.cos(angles) * factor
    basis[FD:, :] = -jnp.sin(angles) * factor

    total = bs[k, lax.rem(q, 2), lax.div(q, 2)]
    for o in range(1, 16):
        scatter_bins(o).wait_recv()
        total = total + br[o]

    traces = jnp.dot(total[:32], basis[...], precision=lax.Precision.HIGHEST, preferred_element_type=F32)
    for part in range(4):
        lag[part] = traces[part * 8 : part * 8 + 8]

    def scatter_x(o):
        return pltpu.make_async_remote_copy(
            src_ref=lag.at[lax.rem(x + o, 4)], dst_ref=xr.at[o],
            send_sem=xr_s.at[o], recv_sem=xr_r.at[o], device_id=x_dev(o), device_id_type=MESH)

    def swap_z(o):
        return pltpu.make_async_remote_copy(
            src_ref=zsum, dst_ref=zr.at[o],
            send_sem=zr_s.at[o], recv_sem=zr_r.at[o], device_id=z_dev(o), device_id_type=MESH)

    def gather_x(o):
        return pltpu.make_async_remote_copy(
            src_ref=fin.at[x], dst_ref=fin.at[x],
            send_sem=fx_s.at[o], recv_sem=fx_r.at[o], device_id=x_dev(o), device_id_type=MESH)

    for o in range(1, 4):
        scatter_x(o).start()
    rows = lag[x]
    for o in range(1, 4):
        scatter_x(o).wait_recv()
        rows = rows + xr[o]
    zsum[...] = rows
    for o in range(1, 4):
        swap_z(o).start()
    counts = jnp.sum(jnp.where(diagonal, total[32:33], 0.0), axis=1, keepdims=True)
    norm_ref[...] = jnp.broadcast_to(jnp.sqrt(jnp.maximum(counts, 1.0)), (32, NLAG))
    for o in range(1, 4):
        swap_z(o).wait_recv()
        rows = rows + zr[o]
    fin[x] = rows
    for o in range(1, 4):
        gather_x(o).start()

    for t in range(T):
        core_src(t).wait_send()
        share_src(t, 0, k).wait_send()

        @pl.loop(1, 16)
        def _(o):
            share_src(t, o, k).wait_send()
            scatter_src(t, o).wait_send()
            gather_src(t, o).wait_send()

    for g in range(2):
        core_bins(g).wait_send()

    @pl.loop(1, 16)
    def _(o):
        scatter_bins(o).wait_send()

    for o in range(1, 4):
        scatter_x(o).wait_send()
        swap_z(o).wait_send()
    for o in range(1, 4):
        gather_x(o).wait()
    out_ref[...] = fin[...]


def body(spectra, src_ids, pair_bin, slot_of_bin):
    vmem = pl.BlockSpec(memory_space=pltpu.VMEM)
    dma = pltpu.SemaphoreType.DMA
    sums, norm = pl.pallas_call(
        kernel,
        out_shape=[jax.ShapeDtypeStruct((4, 8, NLAG), F32), jax.ShapeDtypeStruct((32, NLAG), F32)],
        in_specs=[pl.BlockSpec(memory_space=pltpu.SMEM), pl.BlockSpec(memory_space=pl.ANY), vmem, vmem],
        out_specs=[vmem, vmem],
        scratch_shapes=[
            pltpu.VMEM((2, W, FD, C), BF),
            pltpu.VMEM((64 * FD, C), F32),
            pltpu.VMEM((32, 2 * 64, C), BF),
            pltpu.VMEM((32, 2 * 64, C), BF),
            pltpu.VMEM((T * NS, C), F32),
            pltpu.VMEM((T, 32, NS, C), BF),
            pltpu.VMEM((T, 16, NS, C), BF),
            pltpu.VMEM((T, 16, NS, C), BF),
            pltpu.VMEM((T, 32, NS, C), BF),
            pltpu.VMEM((NBIN, C), jnp.int32),
            pltpu.VMEM((8, NBIN, 8 * C), BF),
            pltpu.VMEM((NBIN, C), BF),
            pltpu.VMEM((NS * 2 * FD, C), F32),
            pltpu.VMEM((4, 2 * C, 8 * C), BF),
            pltpu.VMEM((2 * FD, NLAG), F32),
            pltpu.VMEM((2, 2, 8, 33, C), F32),
            pltpu.VMEM((2, 8, 33, C), F32),
            pltpu.VMEM((16, 33, C), F32),
            pltpu.VMEM((4, 8, NLAG), F32),
            pltpu.VMEM((4, 8, NLAG), F32),
            pltpu.VMEM((8, NLAG), F32),
            pltpu.VMEM((4, 8, NLAG), F32),
            pltpu.VMEM((4, 8, NLAG), F32),
            dma, dma((T,)), dma((T,)), dma((T, 16)), dma((T, 16)), dma((T, 16)), dma((T, 16)), dma((T, 16)), dma((T, 16)),
            dma((2,)), dma((2,)), dma((16,)), dma((16,)), dma((4,)), dma((4,)), dma((4,)), dma((4,)), dma((4,)), dma((4,)),
        ],
        compiler_params=pltpu.CompilerParams(
            collective_id=0, has_side_effects=True, vmem_limit_bytes=56 * 1024 * 1024),
    )(src_ids, spectra, pair_bin.reshape(T * NS, C), slot_of_bin.reshape(NBIN // C, C))
    return sums.reshape(32, NLAG) / norm


def solution(mesh):
    return jax.shard_map(
        body,
        mesh=mesh,
        in_specs=(P(None, None, "freq", "chan"), P(), P(None, None, "chan"), P()),
        out_specs=P("chan", None),
        check_vma=False,
    )
```

```python
import math

import jax
import jax.numpy as jnp
from jax import lax
from jax.experimental import pallas as pl
from jax.experimental.pallas import tpu as pltpu
from jax.sharding import PartitionSpec as P

F = 1024
NLAG = 256
NBIN = 1024
W = 30
T = 2
NS = 32
FD = 64
C = 128
MESH = pl.DeviceIdType.MESH
BF = jnp.bfloat16
F32 = jnp.float32
NT = (((1,), (1,)), ((), ()))


def kernel(
    src_ref, spec_hbm, pair_ref, slot_ref, out_ref, norm_ref,
    spec, xf, bw, bt, picker, pk, ck, rk, sk, slots, onehot, cnt, xs, xt, basis,
    bs, bc, br, lag, xr, zsum, zr, fin,
    in_sem, ck_s, ck_r, rk_s, rk_r, ag_s, ag_r, sc_s, sc_r,
    bc_s, bc_r, br_s, br_r, xr_s, xr_r, zr_s, zr_r, fx_s, fx_r,
):
    chan = lax.axis_index("chan")
    freq = lax.axis_index("freq")
    q = lax.div(chan, 2)
    k = lax.rem(chan, 2)
    y, z = lax.div(q, 4), lax.rem(q, 4)
    h, x = lax.div(freq, 4), lax.rem(freq, 4)
    core = {"chan": q * 2 + 1 - k, "freq": freq}

    def chip_at(o):
        return lax.rem(y + lax.div(o, 4), 4) * 4 + lax.rem(z + lax.rem(o, 4), 4)

    def chip_from(o):
        return lax.rem(y + 4 - lax.div(o, 4), 4) * 4 + lax.rem(z + 4 - lax.rem(o, 4), 4)

    def chip_dev(o):
        return {"chan": chip_at(o) * 2 + k, "freq": freq}

    def x_dev(o):
        return {"chan": chan, "freq": h * 4 + lax.rem(x + o, 4)}

    def z_dev(o):
        return {"chan": chan, "freq": lax.rem(h + o, 4) * 4 + x}

    barrier = pltpu.get_barrier_semaphore()

    def greet(dev):
        pl.semaphore_signal(barrier, inc=1, device_id=dev, device_id_type=MESH)

    @pl.loop(1, 4)
    def _(o):
        greet(z_dev(o))
        greet(x_dev(o))

    @pl.loop(1, 16)
    def _(o):
        greet(chip_dev(o))

    greet(core)

    fetch = pltpu.make_async_copy(spec_hbm, spec, in_sem)
    fetch.start()

    lane = lax.broadcasted_iota(jnp.int32, (1, C), 1) + chan * C
    for t in range(T):
        for s in range(NS):
            row = t * NS + s
            picker[row : row + 1, :] = jnp.where(lane == src_ref[t, s], 1.0, 0.0)
    for part in range(2):
        xf[(part * 32 + W) * FD : (part + 1) * 32 * FD, :] = jnp.zeros((2 * FD, C), F32)
    fetch.wait()

    @pl.loop(0, W, unroll=5)
    def _(w):
        for part in range(2):
            at = pl.multiple_of((part * 32 + w) * FD, FD)
            xf[pl.ds(at, FD), :] = spec[part, w].astype(F32)

    pick = picker[...].astype(BF)

    @pl.loop(0, 32, unroll=8)
    def _(fp):
        halves = [xf[pl.ds(par * 32 + fp, 64, stride=FD), :].astype(BF) for par in range(2)]
        b = jnp.concatenate(halves, axis=0)
        bw[fp] = b
        got = lax.dot_general(pick, b, NT, preferred_element_type=F32).astype(BF)
        for t in range(T):
            pk[t, fp] = got[t * NS : (t + 1) * NS]

    pl.semaphore_wait(barrier, 22)

    def core_src(t):
        return pltpu.make_async_remote_copy(
            src_ref=pk.at[t, pl.ds((1 - k) * 16, 16)], dst_ref=ck.at[t],
            send_sem=ck_s.at[t], recv_sem=ck_r.at[t], device_id=core, device_id_type=MESH)

    def scatter_src(t, o):
        return pltpu.make_async_remote_copy(
            src_ref=pk.at[t, k * 16 + chip_at(o)], dst_ref=rk.at[t, o],
            send_sem=rk_s.at[t, o], recv_sem=rk_r.at[t, o], device_id=chip_dev(o), device_id_type=MESH)

    def gather_src(t, o):
        return pltpu.make_async_remote_copy(
            src_ref=sk.at[t, k * 16 + q], dst_ref=sk.at[t, k * 16 + q],
            send_sem=ag_s.at[t, o], recv_sem=ag_r.at[t, o], device_id=chip_dev(o), device_id_type=MESH)

    def share_src(t, o, half):
        at = half * 16 + chip_from(o)
        return pltpu.make_async_remote_copy(
            src_ref=sk.at[t, at], dst_ref=sk.at[t, at],
            send_sem=sc_s.at[t, o], recv_sem=sc_r.at[t, o], device_id=core, device_id_type=MESH)

    for t in range(T):
        core_src(t).start()
    for t in range(T):
        core_src(t).wait_recv()
        mine = pl.ds(k * 16, 16)
        pk[t, mine] = pk[t, mine] + ck[t]

        @pl.loop(1, 16)
        def _(o):
            scatter_src(t, o).start()

    @pl.loop(0, 32, unroll=4)
    def _(fp):
        for par in range(2):
            at = par * 64
            bt[fp, at : at + 32] = bw[fp, at + 32 : at + 64]
            bt[fp, at + 32 : at + 64] = -bw[fp, at : at + 32]

    bin_at = lax.broadcasted_iota(jnp.int32, (NBIN, 2 * C), 0)
    high = lax.broadcasted_iota(jnp.int32, (NBIN, 2 * C), 1) < C
    digits = jnp.where(high, lax.div(bin_at, 32), lax.rem(bin_at, 32)).astype(F32).astype(BF)

    @pl.loop(0, NBIN // C)
    def _(rb):
        at = lax.broadcasted_iota(jnp.int32, (C, C), 0) + rb * C
        chip = lax.div(lax.rem(at, 256), 32) * 2 + lax.div(lax.rem(at, 512), 256)
        rows = chip * 64 + lax.div(at, 512) * 32 + lax.rem(at, 32)
        hit = jnp.concatenate(
            [jnp.where(slot_ref[i : i + 1, :] == rows, 1.0, 0.0).astype(BF) for i in range(NBIN // C)], axis=1)
        found = jnp.dot(hit, digits, preferred_element_type=F32)
        at = pl.ds(pl.multiple_of(rb * C, C), C)
        slots[at, :] = (found[:, :C] * 32.0 + found[:, C:]).astype(jnp.int32)
        cnt[at, :] = jnp.zeros((C, C), BF)

    def build_hits(t):
        @pl.loop(0, 4)
        def _(ch):
            @pl.loop(0, NBIN // C)
            def _(rb):
                at = pl.ds(pl.multiple_of(rb * C, C), C)
                held = slots[at, :]
                total = cnt[at, :]
                for i in range(8):
                    row = pair_ref[pl.ds(t * NS + ch * 8 + i, 1), :]
                    hit = jnp.where(held == row, 1.0, 0.0).astype(BF)
                    onehot[t * 4 + ch, at, i * C : (i + 1) * C] = hit
                    total = total + hit
                cnt[at, :] = total

    def reduce_src(t):
        total = pk[t, k * 16 + q]
        for o in range(1, 16):
            scatter_src(t, o).wait_recv()
            total = total + rk[t, o]
        sk[t, k * 16 + q] = total

        @pl.loop(1, 16)
        def _(o):
            gather_src(t, o).start()

    build_hits(0)
    reduce_src(0)
    reduce_src(1)
    build_hits(1)

    sums = jnp.dot(cnt[...], jnp.ones((C, C), BF), preferred_element_type=F32)
    diagonal = lax.broadcasted_iota(jnp.int32, (32, C), 0) == lax.broadcasted_iota(jnp.int32, (32, C), 1)
    for owner in range(32):
        line = jnp.sum(jnp.where(diagonal, sums[owner * 32 : owner * 32 + 32], 0.0), axis=0, keepdims=True)
        bs[owner // 16, owner // 8 % 2, owner % 8, 32:33, :] = line

    first = lax.broadcasted_iota(jnp.int32, (NS, C), 1) < 64

    def cross(t, fp):
        a = sk[t, fp]
        zero = jnp.zeros_like(a)
        lhs = jnp.concatenate([jnp.where(first, a, zero), jnp.where(first, zero, a)], axis=0)
        got = jnp.dot(lhs, jnp.concatenate([bw[fp], bt[fp]], axis=1), preferred_element_type=F32)
        for par in range(2):
            for j in range(2):
                xs[pl.ds(j * FD + par * 32 + fp, NS, stride=2 * FD), :] = (
                    got[par * NS : (par + 1) * NS, j * C : (j + 1) * C])

    def core_bins(g):
        return pltpu.make_async_remote_copy(
            src_ref=bs.at[1 - k, g], dst_ref=bc.at[g],
            send_sem=bc_s.at[g], recv_sem=bc_r.at[g], device_id=core, device_id_type=MESH)

    def scatter_bins(o):
        to = chip_at(o)
        return pltpu.make_async_remote_copy(
            src_ref=bs.at[k, lax.rem(to, 2), lax.div(to, 2)], dst_ref=br.at[o],
            send_sem=br_s.at[o], recv_sem=br_r.at[o], device_id=chip_dev(o), device_id_type=MESH)

    def split(t):
        for ch in range(4):
            for i in range(8):
                at = (ch * 8 + i) * 2 * FD
                v = xs[at : at + 2 * FD, :]
                hi = v.astype(BF)
                xt[ch, :C, i * C : (i + 1) * C] = hi
                xt[ch, C:, i * C : (i + 1) * C] = (v - hi.astype(F32)).astype(BF)

    def stack(t, start, rows):
        at = pl.ds(start, rows)
        got = sum(
            lax.dot_general(onehot[t * 4 + ch, at, :], xt[ch], NT, preferred_element_type=F32) for ch in range(4))
        return (got[:, :C] + got[:, C:]).reshape(rows // 32, 32, C)

    share_src(0, 0, k).start()
    for group in range(4):
        members = range(group * 4, group * 4 + 4)
        for o in members:
            if o > 0:
                gather_src(0, o).wait_recv()
                share_src(0, o, k).start()
        for o in members:
            cross(0, k * 16 + chip_from(o))
    for group in range(2):
        members = range(group * 8, group * 8 + 8)
        for o in members:
            share_src(0, o, 1 - k).wait_recv()
        for o in members:
            cross(0, (1 - k) * 16 + chip_from(o))

    share_src(1, 0, k).start()

    @pl.loop(1, 16)
    def _(o):
        gather_src(1, o).wait_recv()
        share_src(1, o, k).start()

    split(0)
    part = stack(0, 0, NBIN)
    for n in range(4):
        bs[n // 2, n % 2, :, :32, :] = part[n * 8 : n * 8 + 8]

    for o in range(16):
        cross(1, k * 16 + chip_from(o))

    @pl.loop(0, 16)
    def _(o):
        share_src(1, o, 1 - k).wait_recv()

    for o in range(16):
        cross(1, (1 - k) * 16 + chip_from(o))
    split(1)

    def stack_on(half, g):
        part = stack(1, pl.multiple_of(half * 512 + g * 256, 256), 256)
        bs[half, g, :, :32, :] = bs[half, g, :, :32, :] + part

    for g in range(2):
        stack_on(1 - k, g)
        core_bins(g).start()
        stack_on(k, g)
        core_bins(g).wait_recv()
        bs[k, g] = bs[k, g] + bc[g]

        @pl.loop(0, 8)
        def _(n):
            o = lax.div(n, 2) * 4 + lax.rem(n, 2) * 2 + lax.rem(z + g, 2)

            @pl.when(o > 0)
            def _():
                scatter_bins(o).start()

    tone = lax.broadcasted_iota(jnp.int32, (FD, NLAG), 0) + freq * FD
    shift = lax.broadcasted_iota(jnp.int32, (FD, NLAG), 1) - NLAG // 2
    angles = ((tone * shift) & (2 * F - 1)).astype(F32) * (math.pi / F)
    factor = 1.0 / math.sqrt(W * F)
    table = jnp.concatenate([jnp.cos(angles), -jnp.sin(angles)], axis=0) * factor
    high = table.astype(BF)
    basis[:, :NLAG] = high
    basis[:, NLAG:] = (table - high.astype(F32)).astype(BF)

    total = bs[k, lax.rem(q, 2), lax.div(q, 2)]
    for o in range(1, 16):
        scatter_bins(o).wait_recv()
        total = total + br[o]

    stacks = total[:32]
    stacks_hi = stacks.astype(BF)
    stacks_lo = (stacks - stacks_hi.astype(F32)).astype(BF)
    both = jnp.concatenate([stacks_hi, stacks_lo], axis=0)
    got = jnp.dot(both, basis[...], preferred_element_type=F32)
    traces = got[:32, :NLAG] + (got[32:, :NLAG] + got[:32, NLAG:]) + got[32:, NLAG:]
    for part in range(4):
        lag[part] = traces[part * 8 : part * 8 + 8]

    def scatter_x(o):
        return pltpu.make_async_remote_copy(
            src_ref=lag.at[lax.rem(x + o, 4)], dst_ref=xr.at[o],
            send_sem=xr_s.at[o], recv_sem=xr_r.at[o], device_id=x_dev(o), device_id_type=MESH)

    def swap_z(o):
        return pltpu.make_async_remote_copy(
            src_ref=zsum, dst_ref=zr.at[o],
            send_sem=zr_s.at[o], recv_sem=zr_r.at[o], device_id=z_dev(o), device_id_type=MESH)

    def gather_x(o):
        return pltpu.make_async_remote_copy(
            src_ref=fin.at[x], dst_ref=fin.at[x],
            send_sem=fx_s.at[o], recv_sem=fx_r.at[o], device_id=x_dev(o), device_id_type=MESH)

    for o in range(1, 4):
        scatter_x(o).start()
    rows = lag[x]
    for o in range(1, 4):
        scatter_x(o).wait_recv()
        rows = rows + xr[o]
    zsum[...] = rows
    for o in range(1, 4):
        swap_z(o).start()
    counts = jnp.sum(jnp.where(diagonal, total[32:33], 0.0), axis=1, keepdims=True)
    norm_ref[...] = jnp.broadcast_to(jnp.sqrt(jnp.maximum(counts, 1.0)), (32, NLAG))
    for o in range(1, 4):
        swap_z(o).wait_recv()
        rows = rows + zr[o]
    fin[x] = rows
    for o in range(1, 4):
        gather_x(o).start()

    for t in range(T):
        core_src(t).wait_send()
        share_src(t, 0, k).wait_send()

        @pl.loop(1, 16)
        def _(o):
            share_src(t, o, k).wait_send()
            scatter_src(t, o).wait_send()
            gather_src(t, o).wait_send()

    for g in range(2):
        core_bins(g).wait_send()

    @pl.loop(1, 16)
    def _(o):
        scatter_bins(o).wait_send()

    for o in range(1, 4):
        scatter_x(o).wait_send()
        swap_z(o).wait_send()
    for o in range(1, 4):
        gather_x(o).wait()
    out_ref[...] = fin[...]


def body(spectra, src_ids, pair_bin, slot_of_bin):
    vmem = pl.BlockSpec(memory_space=pltpu.VMEM)
    dma = pltpu.SemaphoreType.DMA
    sums, norm = pl.pallas_call(
        kernel,
        out_shape=[jax.ShapeDtypeStruct((4, 8, NLAG), F32), jax.ShapeDtypeStruct((32, NLAG), F32)],
        in_specs=[pl.BlockSpec(memory_space=pltpu.SMEM), pl.BlockSpec(memory_space=pl.ANY), vmem, vmem],
        out_specs=[vmem, vmem],
        scratch_shapes=[
            pltpu.VMEM((2, W, FD, C), BF),
            pltpu.VMEM((64 * FD, C), F32),
            pltpu.VMEM((32, 2 * 64, C), BF),
            pltpu.VMEM((32, 2 * 64, C), BF),
            pltpu.VMEM((T * NS, C), F32),
            pltpu.VMEM((T, 32, NS, C), BF),
            pltpu.VMEM((T, 16, NS, C), BF),
            pltpu.VMEM((T, 16, NS, C), BF),
            pltpu.VMEM((T, 32, NS, C), BF),
            pltpu.VMEM((NBIN, C), jnp.int32),
            pltpu.VMEM((8, NBIN, 8 * C), BF),
            pltpu.VMEM((NBIN, C), BF),
            pltpu.VMEM((NS * 2 * FD, C), F32),
            pltpu.VMEM((4, 2 * C, 8 * C), BF),
            pltpu.VMEM((2 * FD, 2 * NLAG), BF),
            pltpu.VMEM((2, 2, 8, 33, C), F32),
            pltpu.VMEM((2, 8, 33, C), F32),
            pltpu.VMEM((16, 33, C), F32),
            pltpu.VMEM((4, 8, NLAG), F32),
            pltpu.VMEM((4, 8, NLAG), F32),
            pltpu.VMEM((8, NLAG), F32),
            pltpu.VMEM((4, 8, NLAG), F32),
            pltpu.VMEM((4, 8, NLAG), F32),
            dma, dma((T,)), dma((T,)), dma((T, 16)), dma((T, 16)), dma((T, 16)), dma((T, 16)), dma((T, 16)), dma((T, 16)),
            dma((2,)), dma((2,)), dma((16,)), dma((16,)), dma((4,)), dma((4,)), dma((4,)), dma((4,)), dma((4,)), dma((4,)),
        ],
        compiler_params=pltpu.CompilerParams(
            collective_id=0, has_side_effects=True, vmem_limit_bytes=56 * 1024 * 1024),
    )(src_ids, spectra, pair_bin.reshape(T * NS, C), slot_of_bin.reshape(NBIN // C, C))
    return sums.reshape(32, NLAG) / norm


def solution(mesh):
    return jax.shard_map(
        body,
        mesh=mesh,
        in_specs=(P(None, None, "freq", "chan"), P(), P(None, None, "chan"), P()),
        out_specs=P("chan", None),
        check_vma=False,
    )
```
